256 devices in a mesh: row: 64 (over y, z, core), col: 4 (over x).
Axes of the slice: x: 4, y: 4, z: 8, core: 2. Of those that a mesh axis runs over, the one named last changes fastest.
Arguments:
- matrix: bfloat16 [8192, 65536], P('col', 'row'), may hold values from -6 to 6
- prev_lower: bfloat16 [8192, 512], P('col'), may hold values from -1.1953125 to 1.1953125
- prev_upper: bfloat16 [512, 65536], P(None, 'row'), may hold values from -1.1953125 to 1.1953125
- lower_inverse: bfloat16 [512, 512], P('row'), as said below
- upper_inverse: bfloat16 [512, 512], P('col'), as said below
Outputs:
- factored: bfloat16 [8192, 65536], P('col', 'row')
The draws below stay inside these ranges and needn't reach their ends.
Inputs may be any that keep to these rules, and one draw needn't show every extreme that they name: lower_inverse is unit lower triangular. upper_inverse is upper triangular with a positive diagonal.
All inputs are finite; a program needn't handle non-finite values.
Results may differ from the reference program's by a relative error of at most 0.0058.
Values may be sent and summed in bfloat16 or wider, within the bound.
A program may use at most 64 MiB of HBM per device.

```python
import math
import jax
import jax.numpy as jnp
from jax import lax

NB = 512
MC = 1024
ROWS = 8192
COLS = 65536
N_ROW = 64


def draw_lower_inverse(key, part):
    values = jax.random.normal(key, (NB, NB), jnp.float32) * (0.5 / math.sqrt(NB))
    row_index = jnp.arange(NB)[:, None]
    col_index = jnp.arange(NB)[None, :]
    return jnp.where(row_index > col_index, values, jnp.where(row_index == col_index, 1.0, 0.0)).astype(jnp.bfloat16)


def draw_upper_inverse(key, part):
    first_key = jax.random.fold_in(key, 11)
    second_key = jax.random.fold_in(key, 23)
    values = jax.random.normal(first_key, (NB, NB), jnp.float32) * (0.03 / math.sqrt(NB))
    diagonal = jnp.exp(jax.random.uniform(second_key, (NB,), jnp.float32, math.log(0.01), math.log(0.05)))
    row_index = jnp.arange(NB)[:, None]
    col_index = jnp.arange(NB)[None, :]
    return jnp.where(row_index < col_index, values, jnp.where(row_index == col_index, diagonal[None, :], 0.0)).astype(jnp.bfloat16)


def shard_levels(rng, dims, pieces, smallest, top_value):
    def one(position, parts):
        steps = jax.random.uniform(jax.random.fold_in(jax.random.fold_in(rng, 6), position), (parts,), jnp.float32, smallest / len(pieces), top_value / len(pieces))
        return jnp.repeat(jnp.exp(steps), dims[position] // parts).reshape((-1,) + (1,) * (len(dims) - position - 1))

    factor_of = one(*pieces[0])
    for cut in pieces[1:]:
        factor_of = factor_of * one(*cut)
    return factor_of


def gaussian(own_key, dims, deviation, bound, cuts=(), kind=jnp.bfloat16):
    loudness = shard_levels(own_key, dims, cuts, -0.22, 0.18) if cuts else 1.0
    values = jax.random.normal(own_key, dims, jnp.float32) * deviation * loudness
    return jnp.minimum(jnp.maximum(values, -bound), bound).astype(kind)


def setup_inputs(seed: int = 0) -> dict:
    key_list = jax.random.split(jax.random.key(seed), 6)
    return {
        "matrix": gaussian(key_list[0], (ROWS, COLS), 1.0, 6.0, ((0, 4), (1, 64))),
        "prev_lower": gaussian(key_list[1], (ROWS, NB), 0.2, 1.1953125, ((0, 4),)),
        "prev_upper": gaussian(key_list[2], (NB, COLS), 0.2, 1.1953125, ((1, 64),)),
        "lower_inverse": draw_lower_inverse(jax.random.fold_in(key_list[5], 71), 0),
        "upper_inverse": draw_upper_inverse(jax.random.fold_in(key_list[5], 71), 0),
    }


def reference(matrix, prev_lower, prev_upper, lower_inverse, upper_inverse):
    lower_panel = jnp.dot(matrix[NB:, :NB], upper_inverse, preferred_element_type=jnp.float32).astype(jnp.bfloat16)
    lower_wide = jnp.pad(lower_panel, ((0, 0), (0, MC - NB)))

    def column_block(block_index, result):
        col_start = (jnp.asarray(block_index).astype(jnp.int32) * MC).astype(jnp.int32)
        columns = lax.dynamic_slice_in_dim(matrix, col_start, MC, 1)
        upper_cols = lax.dynamic_slice_in_dim(prev_upper, col_start, MC, 1)
        product = jnp.dot(prev_lower, upper_cols, preferred_element_type=jnp.float32)
        refreshed = (columns.astype(jnp.float32) - product).astype(jnp.bfloat16)
        refreshed = lax.optimization_barrier(refreshed)
        band_mask = (jnp.arange(MC, dtype=jnp.int32)[None, :] + col_start) < NB
        upper_row = jnp.dot(lower_inverse, refreshed[:NB], preferred_element_type=jnp.float32).astype(jnp.bfloat16)
        update = jnp.dot(lower_panel, upper_row, preferred_element_type=jnp.float32)
        trailing = (refreshed[NB:].astype(jnp.float32) - update).astype(jnp.bfloat16)
        top_block = jnp.where(band_mask, columns[:NB], upper_row)
        bottom_block = jnp.where(band_mask, lower_wide, trailing)
        joined = jnp.concatenate([top_block, bottom_block], 0)
        return lax.dynamic_update_slice_in_dim(result, joined, col_start, 1)

    return lax.fori_loop(0, N_ROW, column_block, jnp.zeros((ROWS, COLS), jnp.bfloat16))
```

```python
import functools

import jax
import jax.numpy as jnp
from jax import lax
from jax.experimental import pallas as pl
from jax.experimental.pallas import tpu as pltpu
from jax.sharding import PartitionSpec as P

MESH = pl.DeviceIdType.MESH
NY, NZ, NX = 4, 8, 4
NB = 512
CH = 64
HOP = 3
EARLY = 3
F32 = jnp.float32
BF16 = jnp.bfloat16


def dot(a, b):
    return jnp.dot(a, b, preferred_element_type=F32)


def device(y, z, k, x):
    row = (lax.rem(y + NY, NY) * NZ + lax.rem(z + NZ, NZ)) * 2 + k
    return (row, lax.rem(x + NX, NX))


def kernel(m_hbm, pl_hbm, pu_hbm, li_hbm, ui_hbm, o_hbm,
           m, prev_l, prev_u, linv, uinv, lp, r0, ur, out,
           in_sem, out_sem, bar_unused, xss, xrs, pss, prs, zss, zrs, yss, yrs, kss, krs, uss, urs):
    rows = m.shape[0]
    n_chunk = rows // CH
    r = lax.axis_index("row")
    c = lax.axis_index("col")
    y, z, k = r // 16, (r // 2) % NZ, r % 2
    top = c == 0
    first = r == 0
    lo = jnp.where(top, NB // CH, 0)

    own_l = linv.at[y, z, k]
    loads = [
        pltpu.make_async_copy(li_hbm, own_l, in_sem.at[0]),
        pltpu.make_async_copy(ui_hbm, uinv.at[c], in_sem.at[1]),
        pltpu.make_async_copy(pu_hbm, prev_u, in_sem.at[2]),
        pltpu.make_async_copy(pl_hbm, prev_l, in_sem.at[3]),
        pltpu.make_async_copy(m_hbm, m, in_sem.at[4]),
    ]
    for load in loads:
        load.start()

    barrier = pltpu.get_barrier_semaphore()
    partners = [device(y, z + d, k, c) for d in range(1, NZ)]
    partners += [device(y + d, z, k, c) for d in range(1, NY)]
    partners += [device(y, z, k, c + d) for d in range(1, NX)]
    partners += [device(y, z, 1 - k, c)]
    partners += [device(y + dy, z + dz, 1 - k, c) for dy, dz in ((1, 0), (3, 0), (0, 1), (0, 7))]
    for partner in partners:
        pl.semaphore_signal(barrier, inc=1, device_id=partner, device_id_type=MESH)
    pl.semaphore_wait(barrier, len(partners))

    def remote(src, dst, send, recv, to):
        return pltpu.make_async_remote_copy(src_ref=src, dst_ref=dst, send_sem=send, recv_sem=recv,
                                            device_id=to, device_id_type=MESH)

    loads[0].wait()
    loads[1].wait()
    z_sends = [remote(own_l, own_l, zss.at[d - 1], zrs.at[z], device(y, z + d, k, c)) for d in range(1, NZ)]
    for copy in z_sends:
        copy.start()
    u_sends = [remote(uinv.at[c], uinv.at[c], uss.at[d - 1], urs.at[c], device(y, z, k, c + d)) for d in range(1, NX)]

    @pl.when(first)
    def _():
        for copy in u_sends:
            copy.start()

    loads[2].wait()
    loads[3].wait()
    loads[4].wait()

    def x_chunk(h, n):
        part = r0.at[h, n // 4, pl.ds(pl.multiple_of((n % 4) * 128, 128), 128)]
        to = device(y, z, k, c + 1 if h == 0 else c + 3)
        return remote(part, part, xss.at[h, n], xrs.at[h, n], to)

    @pl.when(top)
    def _():
        for p in range(4):
            for h in range(2):
                cols = slice(h * 512 + p * 128, h * 512 + p * 128 + 128)
                product = dot(prev_l[:NB], prev_u[:, cols])
                r0[h, p] = (m[:NB, cols].astype(F32) - product).astype(BF16)
            for i in range(4):
                for h in range(2):
                    x_chunk(h, 4 * p + i).start()

    def ref_chunk(i):
        return lp.at[pl.ds(pl.multiple_of(i * CH, CH), CH)]

    def p_send(i, d, to):
        return remote(ref_chunk(i), ref_chunk(i), pss.at[d, i], prs.at[i], to)

    def root_sends(i, q):
        kk = i % 2
        sends = {0: [(0, device(1, 0, kk, c))], 1: [(1, device(3, 0, kk, c))],
                 2: [(2, device(0, 1, kk, c)), (3, device(0, 7, kk, c))]}[q]
        return sends + [(4, device(0, 0, 1, c))]

    @pl.when(first)
    def _():
        for d in range(1, NX):
            src = lax.rem(c + d, NX)
            remote(uinv.at[src], uinv.at[src], uss.at[0], urs.at[src], device(y, z, k, c)).wait_recv()
        full = uinv[...].reshape(NB, NB)
        for t in range(rows // 256):
            def block():
                lp[t * 256:(t + 1) * 256] = dot(m[t * 256:(t + 1) * 256, :NB], full).astype(BF16)
                for i in range(t * 256 // CH, (t + 1) * 256 // CH):
                    for d, to in root_sends(i, i % 3):
                        p_send(i, d, to).start()
            if t * 256 < NB:
                pl.when(jnp.logical_not(top))(block)
            else:
                block()

    az = jnp.minimum(z, NZ - z)
    grow_up = z <= 3
    grow_down = jnp.logical_or(z == 0, jnp.logical_or(z == 6, z == 7))
    yes = {0: [], 1: [], 2: []}
    depth = []
    for q in range(2):
        yq = y if q == 0 else lax.rem(NY - y, NY)
        depth.append(az + jnp.where(yq == 1, 1, jnp.where(yq == 3, 3, 2)))
        at1 = yq == 1
        up = (0, 1) if q == 0 else (1, 0)
        fwd = jnp.logical_or(at1, yq == 2)
        back = jnp.logical_and(at1, z != 0)
        conds = [None] * 4
        conds[up[0]] = fwd
        conds[up[1]] = back
        conds[2] = jnp.logical_and(at1, grow_up)
        conds[3] = jnp.logical_and(at1, grow_down)
        yes[q] = conds
    dy = jnp.minimum(y, NY - y)
    depth.append(jnp.where(z == 0, dy + 2, az + dy))
    at0 = jnp.logical_and(y == 0, z != 0)
    yes[2] = [at0, at0, jnp.logical_and(y == 0, grow_up),
              jnp.logical_or(jnp.logical_and(y == 0, grow_down), jnp.logical_and(y != 0, z == 1))]
    one = jnp.logical_and(y == 1, z != 0)
    three = jnp.logical_and(y == 3, z != 0)
    root_chip = jnp.logical_and(y == 0, z == 0)

    def tree_sends(q, n, i):
        conds = list(yes[q])
        if q == 2:
            turn = (n // 2) % 2
            conds[0] = jnp.logical_or(conds[0], jnp.logical_and(one, turn == 0))
            conds[1] = jnp.logical_or(conds[1], jnp.logical_and(three, turn == 1))
        targets = [device(y + 1, z, k, c), device(y + 3, z, k, c), device(y, z + 1, k, c), device(y, z + 7, k, c)]
        sends = [(conds[d], p_send(i, d, targets[d])) for d in range(4)]
        sends.append((i >= 0, p_send(i, 4, device(y, z, 1 - k, c))))
        return sends

    def relays(n, q):
        i = 3 * n + q
        ok = jnp.logical_and(jnp.logical_and(i >= lo, i < n_chunk), jnp.logical_and(i % 2 == k, jnp.logical_not(root_chip)))
        return i, ok

    y_sends = [remote(linv.at[y, :, k], linv.at[y, :, k], yss.at[d - 1], yrs.at[y], device(y + d, z, k, c))
               for d in range(1, NY)]
    k_send = remote(linv.at[:, :, k], linv.at[:, :, k], kss.at[0], krs.at[0], device(y, z, 1 - k, c))

    n_x = 16
    steps = max(n_x + 3 * HOP, EARLY + 7 * HOP + n_chunk // 3 + 2)

    @pl.loop(0, steps)
    def _(s):
        @pl.when(s == 5)
        def _():
            for d in range(1, NZ):
                src = lax.rem(z + d, NZ)
                remote(own_l, linv.at[y, src, k], zss.at[0], zrs.at[src], device(y, z + 1, k, c)).wait_recv()
            for copy in y_sends:
                copy.start()

        @pl.when(s == 11)
        def _():
            for d in range(1, NY):
                src = lax.rem(y + d, NY)
                remote(linv.at[src, :, k], linv.at[src, :, k], yss.at[0], yrs.at[src],
                       device(y + 1, z, k, c)).wait_recv()
            k_send.start()

        for h in range(2):
            hop = c if h == 0 else lax.rem(NX - c, NX)
            n = s - HOP * (hop - 1)
            live = jnp.logical_and(jnp.logical_not(top), jnp.logical_and(n >= 0, n < n_x))

            @pl.when(live)
            def _():
                x_chunk(h, n).wait_recv()

            @pl.when(jnp.logical_and(live, hop < 3))
            def _():
                x_chunk(h, n).start()

        for q in range(3):
            n = s - EARLY - HOP * (depth[q] - 1) + jnp.where(top, 2, 0)
            i, ok = relays(n, q)

            @pl.when(ok)
            def _():
                p_send(i, 0, device(y + 1, z, k, c)).wait_recv()
                for cond, copy in tree_sends(q, n, i):
                    pl.when(cond)(copy.start)

        @pl.when(s < rows // 256)
        def _():
            tile = pl.ds(pl.multiple_of(s * 256, 256), 256)
            out[tile] = (m[tile].astype(F32) - dot(prev_l[tile], prev_u[...])).astype(BF16)

    @pl.loop(0, n_chunk)
    def _(i):
        mine = jnp.logical_and(i % 2 == k, jnp.logical_not(root_chip))

        @pl.when(jnp.logical_and(jnp.logical_and(i >= lo, jnp.logical_not(mine)), jnp.logical_not(first)))
        def _():
            p_send(i, 4, device(y, z, 1 - k, c)).wait_recv()

    remote(linv.at[:, :, 1 - k], linv.at[:, :, 1 - k], kss.at[0], krs.at[0], device(y, z, 1 - k, c)).wait_recv()

    full_l = linv[...].reshape(NB, NB)
    for p in range(4):
        ur[p] = dot(full_l, jnp.concatenate([r0[0, p], r0[1, p]], axis=1)).astype(BF16)

    stores = [pltpu.make_async_copy(out.at[pl.ds(t * NB, NB)], o_hbm.at[pl.ds(t * NB, NB)], out_sem.at[t])
              for t in range(rows // NB)]
    for t in range(rows // NB):
        tile = slice(t * NB, (t + 1) * NB)

        def body():
            for p in range(4):
                update = dot(lp[tile], ur[p])
                for h in range(2):
                    cols = slice(h * 512 + p * 128, h * 512 + p * 128 + 128)
                    part = update[:, h * 128:(h + 1) * 128]
                    value = (out[tile, cols].astype(F32) - part).astype(BF16)
                    if h == 0:
                        value = jnp.where(first, lp[tile, cols], value)
                    out[tile, cols] = value

        if t == 0:
            @pl.when(top)
            def _():
                for p in range(4):
                    for h in range(2):
                        cols = slice(h * 512 + p * 128, h * 512 + p * 128 + 128)
                        value = ur[p, :, h * 128:(h + 1) * 128]
                        if h == 0:
                            value = jnp.where(first, m[tile, cols], value)
                        out[tile, cols] = value

            pl.when(jnp.logical_not(top))(body)
        else:
            body()
        stores[t].start()

    for copy in z_sends + y_sends + [k_send]:
        copy.wait_send()

    @pl.when(first)
    def _():
        for copy in u_sends:
            copy.wait_send()
        for i in range(n_chunk):
            def done():
                for d, to in root_sends(i, i % 3):
                    p_send(i, d, to).wait_send()
            if i < NB // CH:
                pl.when(jnp.logical_not(top))(done)
            else:
                done()

    @pl.loop(0, n_x)
    def _(n):
        @pl.when(c <= 2)
        def _():
            x_chunk(0, n).wait_send()

        @pl.when(c != 1)
        def _():
            x_chunk(1, n).wait_send()

    @pl.loop(0, (n_chunk + 2) // 3)
    def _(n):
        for q in range(3):
            i, ok = relays(n, q)

            @pl.when(ok)
            def _():
                for cond, copy in tree_sends(q, n, i):
                    pl.when(cond)(copy.wait_send)

    for store in stores:
        store.wait()


def local(matrix, prev_lower, prev_upper, lower_inverse, upper_inverse):
    rows, cols = matrix.shape
    n_chunk = rows // CH
    dma = pltpu.SemaphoreType.DMA
    hbm = pl.BlockSpec(memory_space=pl.ANY)
    return pl.pallas_call(
        kernel,
        name="lu_step",
        out_shape=jax.ShapeDtypeStruct((rows, cols), BF16),
        in_specs=[hbm] * 5,
        out_specs=hbm,
        scratch_shapes=[
            pltpu.VMEM((rows, cols), BF16),
            pltpu.VMEM((rows, NB), BF16),
            pltpu.VMEM((NB, cols), BF16),
            pltpu.VMEM((NY, NZ, 2, 8, NB), BF16),
            pltpu.VMEM((NX, NB // NX, NB), BF16),
            pltpu.VMEM((rows, NB), BF16),
            pltpu.VMEM((2, 4, NB, 128), BF16),
            pltpu.VMEM((4, NB, 256), BF16),
            pltpu.VMEM((rows, cols), BF16),
            dma((5,)),
            dma((rows // NB,)),
            dma((1,)),
            dma((2, 16)),
            dma((2, 16)),
            dma((5, n_chunk)),
            dma((n_chunk,)),
            dma((NZ - 1,)),
            dma((NZ,)),
            dma((NY - 1,)),
            dma((NY,)),
            dma((1,)),
            dma((1,)),
            dma((NX - 1,)),
            dma((NX,)),
        ],
        compiler_params=pltpu.CompilerParams(collective_id=0, has_side_effects=True, vmem_limit_bytes=48 << 20),
        cost_estimate=pl.CostEstimate(flops=6 << 30, bytes_accessed=12 << 20, transcendentals=0),
    )(matrix, prev_lower, prev_upper, lower_inverse, upper_inverse)


def solution(mesh):
    in_specs = (P("col", "row"), P("col", None), P(None, "row"), P("row", None), P("col", None))
    out_specs = P("col", "row")
    return jax.shard_map(local, mesh=mesh, in_specs=in_specs, out_specs=out_specs, check_vma=False)
```

```python
import jax
import jax.numpy as jnp
from jax import lax
from jax.experimental import pallas as pl
from jax.experimental.pallas import tpu as pltpu
from jax.sharding import PartitionSpec as P

MESH = pl.DeviceIdType.MESH
NB = 512
CH = 64
HOP = 4
EARLY = 4
LATE = 4
SOLVE = 4
X_AT = 1
COUNT = (5, 5, 6)
N_X = 16
F32 = jnp.float32
BF16 = jnp.bfloat16


def dot(a, b):
    return jnp.dot(a, b, preferred_element_type=F32)


def both(a, b):
    return jnp.logical_and(a, b)


def either(a, b):
    return jnp.logical_or(a, b)


def remote(src, send, recv, to):
    return pltpu.make_async_remote_copy(src_ref=src, dst_ref=src, send_sem=send, recv_sem=recv,
                                        device_id=to, device_id_type=MESH)


def spread(m_hbm, pl_hbm, pu_hbm, li_hbm, ui_hbm, ref, lp, ur,
           m, prev_l, prev_u, linv, uinv, r0,
           in_sem, xss, xrs, pss, prs, prs2, prs3, zss, zrs, yss, yrs, kss, krs, uss, urs):
    rows = m.shape[0]
    r = lax.axis_index("row")
    c = lax.axis_index("col")
    y, z, k = r // 16, (r // 2) % 8, r % 2
    top = c == 0
    root = r == 0
    root_chip = r < 2

    own_l = linv.at[y, z, k]
    loads = [pltpu.make_async_copy(src, dst, in_sem.at[i]) for i, (src, dst) in enumerate((
        (li_hbm, own_l),
        (ui_hbm, uinv.at[c]),
        (pu_hbm, prev_u),
        (pl_hbm.at[pl.ds(0, NB)], prev_l.at[pl.ds(0, NB)]),
        (m_hbm.at[pl.ds(0, NB)], m.at[pl.ds(0, NB)]),
        (m_hbm.at[pl.ds(NB, rows - NB)], m.at[pl.ds(NB, rows - NB)]),
        (pl_hbm.at[pl.ds(NB, rows - NB)], prev_l.at[pl.ds(NB, rows - NB)]),
    ))]
    for load in loads:
        load.start()

    zs = [r + 2 * d - 16 * ((z + d) // 8) for d in range(1, 8)]
    ys = [r + 16 * d - 64 * ((y + d) // 4) for d in range(1, 4)]
    xs = [(c + d) % 4 for d in range(1, 4)]
    sib = (r + 1 - 2 * k, c)
    zp, zp2, zm2, zm = (zs[0], c), (zs[1], c), (zs[5], c), (zs[6], c)
    yp, ym = (ys[0], c), (ys[2], c)
    xp, xm = (r, xs[0]), (r, xs[2])

    def other(at):
        return (at[0] + 1 - 2 * k, c)

    barrier = pltpu.get_barrier_semaphore()

    def greet(at):
        pl.semaphore_signal(barrier, inc=1, device_id=at, device_id_type=MESH)

    for at in [zp, zm, yp, ym, sib] + [(r, a) for a in xs]:
        if at is zp:
            pl.when(zs[0] != 0)(lambda: greet(zp))
        else:
            greet(at)
    for at in (zp2, zm2):
        pl.when(at[0] != 0)(lambda at=at: greet(at))
    at_root = (0, c)
    for a in (3, 17, 49):
        pl.when(r == a)(lambda: greet(at_root))
    pl.when(r == 14)(lambda: greet((1, c)))
    pl.semaphore_wait(barrier, jnp.where(r == 1, 11, 10))

    loads[0].wait()
    loads[1].wait()

    def z_block(up, t):
        part = linv.at[y, (z - t) % 8 if up else (z + t) % 8, k]
        return remote(part, zss.at[0], zrs.at[0 if up else 1, t], zp if up else zm)

    def z_arrived(up, t):
        return remote(own_l, zss.at[0], zrs.at[0 if up else 1, t - 1], zp)

    def y_slab(up, t):
        part = linv.at[(y - t) % 4, :, k]
        return remote(part, yss.at[0], yrs.at[t if up else 2], yp if up else ym)

    def y_arrived(i):
        return remote(lp.at[pl.ds(0, 64)], yss.at[0], yrs.at[i], yp)

    z_block(True, 0).start()
    pl.when(r != 0)(z_block(False, 0).start)
    u_sends = [remote(uinv.at[c], uss.at[0], urs.at[0], (r, a)) for a in xs]

    @pl.when(root)
    def _():
        for copy in u_sends:
            copy.start()

    def x_chunk(h, n):
        part = r0.at[h, n // 4, pl.ds(pl.multiple_of((n % 4) * 128, 128), 128)]
        return remote(part, xss.at[h], xrs.at[h, n], xp if h == 0 else xm)

    for load in loads[2:5]:
        load.wait()

    @pl.when(top)
    def _():
        for p in range(4):
            cols = [slice(h * 512 + p * 128, h * 512 + p * 128 + 128) for h in range(2)]
            product = dot(prev_l[:NB], jnp.concatenate([prev_u[:, a] for a in cols], axis=1))
            for h in range(2):
                part = product[:, h * 128:(h + 1) * 128]
                r0[h, p] = (m[:NB, cols[h]].astype(F32) - part).astype(BF16)
            for i in range(4):
                for h in range(2):
                    x_chunk(h, 4 * p + i).start()

    for load in loads[5:]:
        load.wait()

    def p_chunk(j, kk):
        return lp.at[pl.ds(pl.multiple_of((2 * j + kk) * CH, CH), CH)]

    def p_send(j, kk, q, slot, to):
        return remote(p_chunk(j, kk), pss.at[q, slot], prs.at[j], to)

    def sib_send(j, kk):
        return remote(p_chunk(j, kk), pss.at[3, 0], prs2.at[0], sib)

    def sib_z_send(n, j, kk):
        return remote(p_chunk(j, kk), pss.at[3, 1], prs3.at[n, kk], sib)

    def place(n):
        return jnp.minimum(3 * n + 2, 15)

    def rows_of(n):
        return lp.at[pl.ds(0, n * CH)]

    def core(kk, at):
        return at if kk == 0 else other(at)

    @pl.when(root)
    def _():
        remote(lp.at[pl.ds(0, 384)], uss.at[0], urs.at[0], xp).wait_recv()
        full = uinv[...].reshape(NB, NB)
        for t in range(rows // 256):
            lp[t * 256:(t + 1) * 256] = dot(m[t * 256:(t + 1) * 256, :NB], full).astype(BF16)
            for j in (2 * t, 2 * t + 1):
                q = 2 if j == 15 else j % 3
                for kk in range(2):
                    p_send(j, kk, q, 0, core(kk, (yp, ym, zp)[q])).start()
                    if q == 2:
                        sib_z_send(5 if j == 15 else j // 3, j, kk).start()
                    else:
                        sib_send(j, kk).start()

    zero = z == 0
    z35 = either(z == 3, z == 5)
    z_later = jnp.where(zero, 0, jnp.where(either(z == 1, z == 7), 3, jnp.where(z35, 7, 10)))
    start = []
    slots = []
    up = either(zero, either(z == 1, z35))
    up_to = (jnp.where(z == 1, zs[1], zs[0]), c)
    down = either(zero, either(z == 7, z == 3))
    down_to = (jnp.where(z == 7, zs[5], zs[6]), c)
    for q in range(2):
        near, far = (1, 3) if q == 0 else (3, 1)
        ahead, back = (yp, ym) if q == 0 else (ym, yp)
        at1 = y == near
        start.append(EARLY + z_later + jnp.where(at1, 0, jnp.where(y == far, 2 * HOP + LATE, jnp.where(y == 0, HOP + LATE, HOP))))
        slots.append([
            (either(at1, y == 2), ahead),
            (both(at1, z != 0), back),
            (both(at1, up), up_to),
            (both(at1, down), down_to),
        ])
    dy = jnp.minimum(y, 4 - y)
    on = both(y == 0, z != 0)
    start.append(EARLY - HOP + jnp.where(zero, 3 + (dy + 1) * HOP + LATE, z_later + dy * HOP + jnp.where(both(y == 2, z != 1), LATE, 0)))
    slots.append([
        (on, yp),
        (on, ym),
        (both(on, up), up_to),
        (either(both(on, down), both(y != 0, z == 1)), down_to),
        (both(either(y == 1, y == 3), z != 0), (jnp.where(y == 1, ys[0], ys[2]), c)),
    ])
    turn = jnp.where(y == 1, 0, 1)
    relay = r >= 2

    k_send = remote(linv.at[:, :, k], kss.at[0], krs.at[0], sib)

    steps = max(SOLVE * 7 + 6, EARLY + 10 + 2 * HOP + LATE + 10 + 1)

    @pl.loop(0, steps)
    def _(s):
        for t in range(1, 5):
            @pl.when(s == SOLVE * t + 1)
            def _(t=t):
                z_arrived(True, t).wait_recv()
                if t == 1:
                    pl.when(root)(z_block(False, 0).start)
                if t < 4:
                    z_block(True, t).start()
                    z_arrived(False, t).wait_recv()
                    if t < 3:
                        z_block(False, t).start()
                else:
                    y_slab(True, 0).start()
                    y_slab(False, 0).start()

        @pl.when(s == SOLVE * 5 + 1)
        def _():
            y_arrived(0).wait_recv()
            y_slab(True, 1).start()
            y_arrived(2).wait_recv()

        @pl.when(s == SOLVE * 6 + 1)
        def _():
            y_arrived(1).wait_recv()
            k_send.start()

        for h in range(2):
            n = s - X_AT - jnp.where(c == 2, HOP, 0)

            @pl.when(both(either(c == 2, c == (1 if h == 0 else 3)), both(n >= 0, n < N_X)))
            def _():
                copy = x_chunk(h, n)
                copy.wait_recv()
                copy.start()

        for q in range(3):
            ahead = s - start[q]
            n = ahead // 2

            @pl.when(both(both(relay, ahead >= 0), both(ahead % 2 == 0, n < COUNT[q])))
            def _():
                j = 3 * n + q if q < 2 else place(n)
                p_send(j, k, q, 0, yp).wait_recv()
                for slot, (cond, to) in enumerate(slots[q]):
                    if slot == 4:
                        cond = both(cond, n % 2 == turn)
                    pl.when(cond)(p_send(j, k, q, slot, to).start)
                sib_send(j, k).start()

        back = s - EARLY + 1

        @pl.when(both(both(r == 1, back >= 0), both(back % 2 == 0, back < 2 * COUNT[2])))
        def _():
            n = back // 2
            for kk in range(2):
                sib_z_send(n, place(n), kk).wait_recv()
                p_send(place(n), kk, 2, 0, other(zm) if kk == 0 else zm).start()

        @pl.when(s < rows // 256)
        def _():
            tile = pl.ds(pl.multiple_of(s * 256, 256), 256)
            ref[tile] = (m[tile].astype(F32) - dot(prev_l[tile], prev_u[...])).astype(BF16)

        @pl.when(s == SOLVE * 7 + 1)
        def _():
            remote(lp.at[pl.ds(0, 256)], kss.at[0], krs.at[0], sib).wait_recv()

        p = s - SOLVE * 7 - 2

        @pl.when(both(p >= 0, p < 4))
        def _():
            for h in range(2):
                @pl.when(c == (3 if h == 0 else 1))
                def _():
                    for i in range(4):
                        x_chunk(h, 4 * p + i).wait_recv()

            full_l = linv[...].reshape(NB, NB)
            ur[p] = dot(full_l, jnp.concatenate([r0[0, p], r0[1, p]], axis=1)).astype(BF16)

    @pl.when(relay)
    def _():
        remote(rows_of(16), pss.at[3, 0], prs2.at[0], sib).wait_recv()

    @pl.when(r == 1)
    def _():
        remote(rows_of(20), pss.at[3, 0], prs2.at[0], sib).wait_recv()
        remote(rows_of(12), pss.at[2, 0], prs.at[0], zm).wait_send()

    @pl.when(both(top, root))
    def _():
        ref[:NB, :NB] = m[:NB, :NB]

    remote(lp.at[pl.ds(0, 56)], zss.at[0], zrs.at[0], zp).wait_send()
    remote(lp.at[pl.ds(0, 192)], yss.at[0], yrs.at[0], yp).wait_send()
    k_send.wait_send()

    @pl.when(c <= 2)
    def _():
        remote(r0.at[0], xss.at[0], xrs.at[0, 0], xp).wait_send()

    @pl.when(c != 1)
    def _():
        remote(r0.at[1], xss.at[1], xrs.at[1, 0], xm).wait_send()

    @pl.when(root)
    def _():
        remote(lp.at[pl.ds(0, 384)], uss.at[0], urs.at[0], xp).wait_send()
        for q in range(3):
            remote(rows_of(2 * COUNT[q]), pss.at[q, 0], prs.at[0], yp).wait_send()
        remote(rows_of(20), pss.at[3, 0], prs2.at[0], sib).wait_send()
        remote(rows_of(12), pss.at[3, 1], prs2.at[0], sib).wait_send()

    @pl.when(relay)
    def _():
        for q in range(3):
            for slot, (cond, to) in enumerate(slots[q]):
                n = 3 if slot == 4 else COUNT[q]
                pl.when(cond)(remote(rows_of(n), pss.at[q, slot], prs.at[0], to).wait_send)
        remote(rows_of(16), pss.at[3, 0], prs2.at[0], sib).wait_send()


def finish(ref, lp, ur, out):
    t = pl.program_id(0)
    size = out.shape[0]
    root = lax.axis_index("row") == 0
    pivot = both(lax.axis_index("col") == 0, t < NB // size)
    tile = pl.ds(pl.multiple_of(t * size, size), size)

    def columns(p, h):
        return slice(h * 512 + p * 128, h * 512 + p * 128 + 128)

    @pl.when(pivot)
    def _():
        for p in range(4):
            for h in range(2):
                value = ur[p, tile, h * 128:(h + 1) * 128]
                if h == 0:
                    value = jnp.where(root, ref[tile, columns(p, h)], value)
                out[:, columns(p, h)] = value

    @pl.when(pivot == False)
    def _():
        left = lp[tile]
        for p in range(4):
            update = dot(left, ur[p])
            for h in range(2):
                part = update[:, h * 128:(h + 1) * 128]
                value = (ref[tile, columns(p, h)].astype(F32) - part).astype(BF16)
                if h == 0:
                    value = jnp.where(root, left[:, columns(p, 0)], value)
                out[:, columns(p, h)] = value


def local(*args):
    rows, cols = args[0].shape
    dma = pltpu.SemaphoreType.DMA
    hbm = pl.BlockSpec(memory_space=pl.ANY)
    vmem = pl.BlockSpec(memory_space=pltpu.VMEM)
    args = [pltpu.with_memory_space_constraint(a, pltpu.MemorySpace.HBM) for a in args]
    ref, lp, ur = pl.pallas_call(
        spread,
        name="spread",
        out_shape=(pltpu.VMEM((rows, cols), BF16), pltpu.VMEM((rows, NB), BF16), pltpu.VMEM((4, NB, 256), BF16)),
        in_specs=[hbm] * 5,
        out_specs=(vmem, vmem, vmem),
        scratch_shapes=[
            pltpu.VMEM((rows, cols), BF16),
            pltpu.VMEM((rows, NB), BF16),
            pltpu.VMEM((NB, cols), BF16),
            pltpu.VMEM((4, 8, 2, 8, NB), BF16),
            pltpu.VMEM((4, NB // 4, NB), BF16),
            pltpu.VMEM((2, 4, NB, 128), BF16),
            dma((7,)),
            dma((2,)),
            dma((2, N_X)),
            dma((4, 5)),
            dma((16,)),
            dma((1,)),
            dma((COUNT[2], 2)),
            dma((1,)), dma((2, 4)),
            dma((1,)), dma((3,)),
            dma((1,)), dma((1,)),
            dma((1,)), dma((1,)),
        ],
        compiler_params=pltpu.CompilerParams(collective_id=0, has_side_effects=True, vmem_limit_bytes=40 << 20),
        cost_estimate=pl.CostEstimate(flops=4 << 30, bytes_accessed=7 << 20, transcendentals=0),
    )(*args)
    size = 256
    return pl.pallas_call(
        finish,
        name="finish",
        grid=(rows // size,),
        out_shape=jax.ShapeDtypeStruct((rows, cols), BF16),
        in_specs=[vmem] * 3,
        out_specs=pl.BlockSpec((size, cols), lambda t: (t, 0)),
        compiler_params=pltpu.CompilerParams(vmem_limit_bytes=16 << 20),
        cost_estimate=pl.CostEstimate(flops=2 << 30, bytes_accessed=4 << 20, transcendentals=0),
    )(ref, lp, ur)


def solution(mesh):
    in_specs = (P("col", "row"), P("col", None), P(None, "row"), P("row", None), P("col", None))
    out_specs = P("col", "row")
    return jax.shard_map(local, mesh=mesh, in_specs=in_specs, out_specs=out_specs, check_vma=False)
```

```python
import jax
import jax.numpy as jnp
from jax import lax
from jax.experimental import pallas as pl
from jax.experimental.pallas import tpu as pltpu
from jax.sharding import PartitionSpec as P

MESH = pl.DeviceIdType.MESH
NB = 512
CH = 64
HOP = 4
EARLY = 2
LATE = 4
SOLVE = 4
X_AT = 3
COUNT = (5, 5, 6)
N_X = 16
F32 = jnp.float32
BF16 = jnp.bfloat16


def dot(a, b):
    return jnp.dot(a, b, preferred_element_type=F32)


def both(a, b):
    return jnp.logical_and(a, b)


def either(a, b):
    return jnp.logical_or(a, b)


def remote(src, send, recv, to):
    return pltpu.make_async_remote_copy(src_ref=src, dst_ref=src, send_sem=send, recv_sem=recv,
                                        device_id=to, device_id_type=MESH)


def spread(m_hbm, pl_hbm, pu_hbm, li_hbm, ui_hbm, ref, lp, ur,
           m, prev_l, prev_u, linv, uinv, r0,
           in_sem, xss, xrs, pss, prs, prs2, prs3, zss, zrs, yss, yrs, kss, krs, uss, urs):
    rows = m.shape[0]
    r = lax.axis_index("row")
    c = lax.axis_index("col")
    y, z, k = r // 16, (r // 2) % 8, r % 2
    top = c == 0
    root = r == 0
    root_chip = r < 2

    own_l = linv.at[y, z, k]
    loads = [pltpu.make_async_copy(src, dst, in_sem.at[i]) for i, (src, dst) in enumerate((
        (li_hbm, own_l),
        (ui_hbm, uinv.at[c]),
        (pu_hbm, prev_u),
        (pl_hbm.at[pl.ds(0, NB)], prev_l.at[pl.ds(0, NB)]),
        (m_hbm.at[pl.ds(0, NB)], m.at[pl.ds(0, NB)]),
        (m_hbm.at[pl.ds(NB, rows - NB)], m.at[pl.ds(NB, rows - NB)]),
        (pl_hbm.at[pl.ds(NB, rows - NB)], prev_l.at[pl.ds(NB, rows - NB)]),
    ))]
    for load in loads:
        load.start()

    zs = [r + 2 * d - 16 * ((z + d) // 8) for d in range(1, 8)]
    ys = [r + 16 * d - 64 * ((y + d) // 4) for d in range(1, 4)]
    xs = [(c + d) % 4 for d in range(1, 4)]
    sib = (r + 1 - 2 * k, c)
    zp, zp2, zm2, zm = (zs[0], c), (zs[1], c), (zs[5], c), (zs[6], c)
    yp, ym = (ys[0], c), (ys[2], c)
    xp, xm = (r, xs[0]), (r, xs[2])

    def other(at):
        return (at[0] + 1 - 2 * k, c)

    barrier = pltpu.get_barrier_semaphore()

    def greet(at):
        pl.semaphore_signal(barrier, inc=1, device_id=at, device_id_type=MESH)

    for at in [zp, zm, yp, ym, sib] + [(r, a) for a in xs]:
        if at is zp:
            pl.when(zs[0] != 0)(lambda: greet(zp))
        else:
            greet(at)
    pl.when(z == 3)(lambda: greet(zm2))
    pl.when(z == 5)(lambda: greet(zp2))
    at_root = (0, c)
    for a in (3, 17, 49):
        pl.when(r == a)(lambda: greet(at_root))
    pl.when(r == 14)(lambda: greet((1, c)))
    count = 8 + jnp.where(either(z == 1, z == 7), 1, 0)
    count = jnp.where(root, 10, jnp.where(r == 1, 9, count))
    pl.semaphore_wait(barrier, count)

    loads[0].wait()
    loads[1].wait()

    def z_block(up, t):
        part = linv.at[y, (z - t) % 8 if up else (z + t) % 8, k]
        return remote(part, zss.at[0], zrs.at[0 if up else 1, t], zp if up else zm)

    def z_arrived(up, t):
        return remote(own_l, zss.at[0], zrs.at[0 if up else 1, t - 1], zp)

    def y_slab(up, t):
        part = linv.at[(y - t) % 4, :, k]
        return remote(part, yss.at[0], yrs.at[t if up else 2], yp if up else ym)

    def y_arrived(i):
        return remote(lp.at[pl.ds(0, 64)], yss.at[0], yrs.at[i], yp)

    z_block(True, 0).start()
    pl.when(r != 0)(z_block(False, 0).start)
    u_sends = [remote(uinv.at[c], uss.at[0], urs.at[0], (r, a)) for a in xs]

    @pl.when(root)
    def _():
        for copy in u_sends:
            copy.start()

    def x_chunk(h, n):
        part = r0.at[h, n // 4, pl.ds(pl.multiple_of((n % 4) * 128, 128), 128)]
        return remote(part, xss.at[h], xrs.at[h, n], xp if h == 0 else xm)

    for load in loads[2:5]:
        load.wait()

    @pl.when(top)
    def _():
        for p in range(4):
            cols = [slice(h * 512 + p * 128, h * 512 + p * 128 + 128) for h in range(2)]
            product = dot(prev_l[:NB], jnp.concatenate([prev_u[:, a] for a in cols], axis=1))
            for h in range(2):
                part = product[:, h * 128:(h + 1) * 128]
                r0[h, p] = (m[:NB, cols[h]].astype(F32) - part).astype(BF16)
            for i in range(4):
                for h in range(2):
                    x_chunk(h, 4 * p + i).start()

    for load in loads[5:]:
        load.wait()

    def p_chunk(j, kk):
        return lp.at[pl.ds(pl.multiple_of((2 * j + kk) * CH, CH), CH)]

    def p_send(j, kk, q, slot, to):
        return remote(p_chunk(j, kk), pss.at[q, slot], prs.at[j], to)

    def sib_send(j, kk):
        return remote(p_chunk(j, kk), pss.at[3, 0], prs2.at[0], sib)

    def sib_z_send(n, j, kk):
        return remote(p_chunk(j, kk), pss.at[3, 1], prs3.at[n, kk], sib)

    def place(n):
        return jnp.minimum(3 * n + 2, 15)

    def rows_of(n):
        return lp.at[pl.ds(0, n * CH)]

    def core(kk, at):
        return at if kk == 0 else other(at)

    @pl.when(root)
    def _():
        remote(lp.at[pl.ds(0, 384)], uss.at[0], urs.at[0], xp).wait_recv()
        full = uinv[...].reshape(NB, NB)
        for t in range(rows // 256):
            lp[t * 256:(t + 1) * 256] = dot(m[t * 256:(t + 1) * 256, :NB], full).astype(BF16)
            for j in (2 * t, 2 * t + 1):
                q = 2 if j == 15 else j % 3
                for kk in range(2):
                    p_send(j, kk, q, 0, core(kk, (yp, ym, zp)[q])).start()
                    if q == 2:
                        sib_z_send(5 if j == 15 else j // 3, j, kk).start()
                    else:
                        sib_send(j, kk).start()

    zero = z == 0
    z35 = either(z == 3, z == 5)
    z_later = jnp.where(zero, 0, jnp.where(either(z == 1, z == 7), 3, jnp.where(z35, 7, 10)))
    start = []
    slots = []
    up = either(zero, either(z == 1, z35))
    up_to = (jnp.where(z == 1, zs[1], zs[0]), c)
    down = either(zero, either(z == 7, z == 3))
    down_to = (jnp.where(z == 7, zs[5], zs[6]), c)
    for q in range(2):
        near, far = (1, 3) if q == 0 else (3, 1)
        ahead, back = (yp, ym) if q == 0 else (ym, yp)
        at1 = y == near
        start.append(EARLY + z_later + jnp.where(at1, 0, jnp.where(y == far, 2 * HOP + LATE, jnp.where(y == 0, HOP + LATE, HOP))))
        slots.append([
            (either(at1, y == 2), ahead),
            (both(at1, z != 0), back),
            (both(at1, up), up_to),
            (both(at1, down), down_to),
        ])
    dy = jnp.minimum(y, 4 - y)
    on = both(y == 0, z != 0)
    start.append(EARLY - HOP + jnp.where(zero, 3 + (dy + 1) * HOP + LATE, z_later + dy * HOP + jnp.where(both(y == 2, z != 1), LATE, 0)))
    slots.append([
        (on, yp),
        (on, ym),
        (both(on, up), up_to),
        (either(both(on, down), both(y != 0, z == 1)), down_to),
        (both(either(y == 1, y == 3), z != 0), (jnp.where(y == 1, ys[0], ys[2]), c)),
    ])
    turn = jnp.where(y == 1, 0, 1)
    relay = r >= 2

    k_send = remote(linv.at[:, :, k], kss.at[0], krs.at[0], sib)

    steps = max(SOLVE * 7 + 6, EARLY + 10 + 2 * HOP + LATE + 10 + 1)

    @pl.loop(0, steps)
    def _(s):
        for t in range(1, 5):
            @pl.when(s == SOLVE * t + 1)
            def _(t=t):
                z_arrived(True, t).wait_recv()
                if t == 1:
                    pl.when(root)(z_block(False, 0).start)
                if t < 4:
                    z_block(True, t).start()
                    z_arrived(False, t).wait_recv()
                    if t < 3:
                        z_block(False, t).start()
                else:
                    y_slab(True, 0).start()
                    y_slab(False, 0).start()

        @pl.when(s == SOLVE * 5 + 1)
        def _():
            y_arrived(0).wait_recv()
            y_slab(True, 1).start()
            y_arrived(2).wait_recv()

        @pl.when(s == SOLVE * 6 + 1)
        def _():
            y_arrived(1).wait_recv()
            k_send.start()

        for h in range(2):
            n = s - X_AT - jnp.where(c == 2, HOP, 0)

            @pl.when(both(either(c == 2, c == (1 if h == 0 else 3)), both(n >= 0, n < N_X)))
            def _():
                copy = x_chunk(h, n)
                copy.wait_recv()
                copy.start()

        for q in range(3):
            ahead = s - start[q]
            n = ahead // 2

            @pl.when(both(both(relay, ahead >= 0), both(ahead % 2 == 0, n < COUNT[q])))
            def _():
                j = 3 * n + q if q < 2 else place(n)
                p_send(j, k, q, 0, yp).wait_recv()
                for slot, (cond, to) in enumerate(slots[q]):
                    if slot == 4:
                        cond = both(cond, n % 2 == turn)
                    pl.when(cond)(p_send(j, k, q, slot, to).start)
                sib_send(j, k).start()

        back = s - EARLY + 1

        @pl.when(both(both(r == 1, back >= 0), both(back % 2 == 0, back < 2 * COUNT[2])))
        def _():
            n = back // 2
            for kk in range(2):
                sib_z_send(n, place(n), kk).wait_recv()
                p_send(place(n), kk, 2, 0, other(zm) if kk == 0 else zm).start()

        @pl.when(s < rows // 256)
        def _():
            tile = pl.ds(pl.multiple_of(s * 256, 256), 256)
            ref[tile] = (m[tile].astype(F32) - dot(prev_l[tile], prev_u[...])).astype(BF16)

        @pl.when(s == SOLVE * 7 + 1)
        def _():
            remote(lp.at[pl.ds(0, 256)], kss.at[0], krs.at[0], sib).wait_recv()

        p = s - SOLVE * 7 - 2

        @pl.when(both(p >= 0, p < 4))
        def _():
            for h in range(2):
                @pl.when(c == (3 if h == 0 else 1))
                def _():
                    for i in range(4):
                        x_chunk(h, 4 * p + i).wait_recv()

            full_l = linv[...].reshape(NB, NB)
            ur[p] = dot(full_l, jnp.concatenate([r0[0, p], r0[1, p]], axis=1)).astype(BF16)

    @pl.when(relay)
    def _():
        remote(rows_of(16), pss.at[3, 0], prs2.at[0], sib).wait_recv()

    @pl.when(r == 1)
    def _():
        remote(rows_of(20), pss.at[3, 0], prs2.at[0], sib).wait_recv()
        remote(rows_of(12), pss.at[2, 0], prs.at[0], zm).wait_send()

    @pl.when(both(top, root))
    def _():
        ref[:NB, :NB] = m[:NB, :NB]

    remote(lp.at[pl.ds(0, 56)], zss.at[0], zrs.at[0], zp).wait_send()
    remote(lp.at[pl.ds(0, 192)], yss.at[0], yrs.at[0], yp).wait_send()
    k_send.wait_send()

    @pl.when(c <= 2)
    def _():
        remote(r0.at[0], xss.at[0], xrs.at[0, 0], xp).wait_send()

    @pl.when(c != 1)
    def _():
        remote(r0.at[1], xss.at[1], xrs.at[1, 0], xm).wait_send()

    @pl.when(root)
    def _():
        remote(lp.at[pl.ds(0, 384)], uss.at[0], urs.at[0], xp).wait_send()
        for q in range(3):
            remote(rows_of(2 * COUNT[q]), pss.at[q, 0], prs.at[0], yp).wait_send()
        remote(rows_of(20), pss.at[3, 0], prs2.at[0], sib).wait_send()
        remote(rows_of(12), pss.at[3, 1], prs2.at[0], sib).wait_send()

    @pl.when(relay)
    def _():
        for q in range(3):
            for slot, (cond, to) in enumerate(slots[q]):
                n = 3 if slot == 4 else COUNT[q]
                pl.when(cond)(remote(rows_of(n), pss.at[q, slot], prs.at[0], to).wait_send)
        remote(rows_of(16), pss.at[3, 0], prs2.at[0], sib).wait_send()


def finish(ref, lp, ur, out):
    t = pl.program_id(0)
    size = out.shape[0]
    root = lax.axis_index("row") == 0
    pivot = both(lax.axis_index("col") == 0, t < NB // size)
    tile = pl.ds(pl.multiple_of(t * size, size), size)

    def columns(p, h):
        return slice(h * 512 + p * 128, h * 512 + p * 128 + 128)

    @pl.when(pivot)
    def _():
        for p in range(4):
            for h in range(2):
                value = ur[p, tile, h * 128:(h + 1) * 128]
                if h == 0:
                    value = jnp.where(root, ref[tile, columns(p, h)], value)
                out[:, columns(p, h)] = value

    @pl.when(pivot == False)
    def _():
        left = lp[tile]
        for p in range(4):
            update = dot(left, ur[p])
            for h in range(2):
                part = update[:, h * 128:(h + 1) * 128]
                value = (ref[tile, columns(p, h)].astype(F32) - part).astype(BF16)
                if h == 0:
                    value = jnp.where(root, left[:, columns(p, 0)], value)
                out[:, columns(p, h)] = value


def local(*args):
    rows, cols = args[0].shape
    dma = pltpu.SemaphoreType.DMA
    hbm = pl.BlockSpec(memory_space=pl.ANY)
    vmem = pl.BlockSpec(memory_space=pltpu.VMEM)
    args = [pltpu.with_memory_space_constraint(a, pltpu.MemorySpace.HBM) for a in args]
    ref, lp, ur = pl.pallas_call(
        spread,
        name="spread",
        out_shape=(pltpu.VMEM((rows, cols), BF16), pltpu.VMEM((rows, NB), BF16), pltpu.VMEM((4, NB, 256), BF16)),
        in_specs=[hbm] * 5,
        out_specs=(vmem, vmem, vmem),
        scratch_shapes=[
            pltpu.VMEM((rows, cols), BF16),
            pltpu.VMEM((rows, NB), BF16),
            pltpu.VMEM((NB, cols), BF16),
            pltpu.VMEM((4, 8, 2, 8, NB), BF16),
            pltpu.VMEM((4, NB // 4, NB), BF16),
            pltpu.VMEM((2, 4, NB, 128), BF16),
            dma((7,)),
            dma((2,)),
            dma((2, N_X)),
            dma((4, 5)),
            dma((16,)),
            dma((1,)),
            dma((COUNT[2], 2)),
            dma((1,)), dma((2, 4)),
            dma((1,)), dma((3,)),
            dma((1,)), dma((1,)),
            dma((1,)), dma((1,)),
        ],
        compiler_params=pltpu.CompilerParams(collective_id=0, has_side_effects=True, vmem_limit_bytes=40 << 20),
        cost_estimate=pl.CostEstimate(flops=4 << 30, bytes_accessed=7 << 20, transcendentals=0),
    )(*args)
    size = 512
    return pl.pallas_call(
        finish,
        name="finish",
        grid=(rows // size,),
        out_shape=jax.ShapeDtypeStruct((rows, cols), BF16),
        in_specs=[vmem] * 3,
        out_specs=pl.BlockSpec((size, cols), lambda t: (t, 0)),
        compiler_params=pltpu.CompilerParams(vmem_limit_bytes=16 << 20),
        cost_estimate=pl.CostEstimate(flops=2 << 30, bytes_accessed=4 << 20, transcendentals=0),
    )(ref, lp, ur)


def solution(mesh):
    in_specs = (P("col", "row"), P("col", None), P(None, "row"), P("row", None), P("col", None))
    out_specs = P("col", "row")
    return jax.shard_map(local, mesh=mesh, in_specs=in_specs, out_specs=out_specs, check_vma=False)
```

```python
import jax
import jax.numpy as jnp
from jax import lax
from jax.experimental import pallas as pl
from jax.experimental.pallas import tpu as pltpu
from jax.sharding import PartitionSpec as P

MESH = pl.DeviceIdType.MESH
NB = 512
CH = 32
HOP = 4
EARLY = 2
LATE = 2
SOLVE = 4
X_AT = 3
COUNT = (10, 10, 12)
N_X = 16
F32 = jnp.float32
BF16 = jnp.bfloat16


def dot(a, b):
    return jnp.dot(a, b, preferred_element_type=F32)


def both(a, b):
    return jnp.logical_and(a, b)


def either(a, b):
    return jnp.logical_or(a, b)


def remote(src, send, recv, to):
    return pltpu.make_async_remote_copy(src_ref=src, dst_ref=src, send_sem=send, recv_sem=recv,
                                        device_id=to, device_id_type=MESH)


def spread(m_hbm, pl_hbm, pu_hbm, li_hbm, ui_hbm, ref, lp, ur,
           m, prev_l, prev_u, linv, uinv, r0,
           in_sem, xss, xrs, pss, prs, prs2, prs3, zss, zrs, yss, yrs, kss, krs, uss, urs):
    rows = m.shape[0]
    r = lax.axis_index("row")
    c = lax.axis_index("col")
    y, z, k = r // 16, (r // 2) % 8, r % 2
    top = c == 0
    root = r == 0
    root_chip = r < 2

    own_l = linv.at[y, z, k]
    loads = [pltpu.make_async_copy(src, dst, in_sem.at[i]) for i, (src, dst) in enumerate((
        (li_hbm, own_l),
        (ui_hbm, uinv.at[c]),
        (pu_hbm, prev_u),
        (pl_hbm.at[pl.ds(0, NB)], prev_l.at[pl.ds(0, NB)]),
        (m_hbm.at[pl.ds(0, NB)], m.at[pl.ds(0, NB)]),
        (m_hbm.at[pl.ds(NB, rows - NB)], m.at[pl.ds(NB, rows - NB)]),
        (pl_hbm.at[pl.ds(NB, rows - NB)], prev_l.at[pl.ds(NB, rows - NB)]),
    ))]
    for load in loads:
        load.start()

    zs = [r + 2 * d - 16 * ((z + d) // 8) for d in range(1, 8)]
    ys = [r + 16 * d - 64 * ((y + d) // 4) for d in range(1, 4)]
    xs = [(c + d) % 4 for d in range(1, 4)]
    sib = (r + 1 - 2 * k, c)
    zp, zp2, zm2, zm = (zs[0], c), (zs[1], c), (zs[5], c), (zs[6], c)
    yp, ym = (ys[0], c), (ys[2], c)
    xp, xm = (r, xs[0]), (r, xs[2])

    def other(at):
        return (at[0] + 1 - 2 * k, c)

    barrier = pltpu.get_barrier_semaphore()

    def greet(at):
        pl.semaphore_signal(barrier, inc=1, device_id=at, device_id_type=MESH)

    for at in [zp, zm, yp, ym, sib] + [(r, a) for a in xs]:
        if at is zp:
            pl.when(zs[0] != 0)(lambda: greet(zp))
        else:
            greet(at)
    pl.when(z == 3)(lambda: greet(zm2))
    pl.when(z == 5)(lambda: greet(zp2))
    at_root = (0, c)
    for a in (3, 17, 49):
        pl.when(r == a)(lambda: greet(at_root))
    pl.when(r == 14)(lambda: greet((1, c)))
    count = 8 + jnp.where(either(z == 1, z == 7), 1, 0)
    count = jnp.where(root, 10, jnp.where(r == 1, 9, count))
    pl.semaphore_wait(barrier, count)

    loads[0].wait()
    loads[1].wait()

    def z_block(up, t):
        part = linv.at[y, (z - t) % 8 if up else (z + t) % 8, k]
        return remote(part, zss.at[0], zrs.at[0 if up else 1, t], zp if up else zm)

    def z_arrived(up, t):
        return remote(own_l, zss.at[0], zrs.at[0 if up else 1, t - 1], zp)

    def y_slab(up, t):
        part = linv.at[(y - t) % 4, :, k]
        return remote(part, yss.at[0], yrs.at[t if up else 2], yp if up else ym)

    def y_arrived(i):
        return remote(lp.at[pl.ds(0, 64)], yss.at[0], yrs.at[i], yp)

    z_block(True, 0).start()
    pl.when(r != 0)(z_block(False, 0).start)
    u_sends = [remote(uinv.at[c], uss.at[0], urs.at[0], (r, a)) for a in xs]

    @pl.when(root)
    def _():
        for copy in u_sends:
            copy.start()

    def x_chunk(h, n):
        part = r0.at[h, n // 4, pl.ds(pl.multiple_of((n % 4) * 128, 128), 128)]
        return remote(part, xss.at[h], xrs.at[h, n], xp if h == 0 else xm)

    for load in loads[2:5]:
        load.wait()

    @pl.when(top)
    def _():
        for p in range(4):
            cols = [slice(h * 512 + p * 128, h * 512 + p * 128 + 128) for h in range(2)]
            product = dot(prev_l[:NB], jnp.concatenate([prev_u[:, a] for a in cols], axis=1))
            for h in range(2):
                part = product[:, h * 128:(h + 1) * 128]
                r0[h, p] = (m[:NB, cols[h]].astype(F32) - part).astype(BF16)
            for i in range(4):
                for h in range(2):
                    x_chunk(h, 4 * p + i).start()

    for load in loads[5:]:
        load.wait()

    def p_chunk(j, kk):
        return lp.at[pl.ds(pl.multiple_of((2 * j + kk) * CH, CH), CH)]

    def p_send(j, kk, q, slot, to):
        return remote(p_chunk(j, kk), pss.at[q, slot], prs.at[j], to)

    def sib_send(j, kk):
        return remote(p_chunk(j, kk), pss.at[3, 0], prs2.at[0], sib)

    def sib_z_send(n, j, kk):
        return remote(p_chunk(j, kk), pss.at[3, 1], prs3.at[n, kk], sib)

    def place(n):
        return jnp.where(n < 10, 3 * n + 2, n + 20)

    def rows_of(n):
        return lp.at[pl.ds(0, n * CH)]

    def core(kk, at):
        return at if kk == 0 else other(at)

    @pl.when(root)
    def _():
        remote(lp.at[pl.ds(0, 384)], uss.at[0], urs.at[0], xp).wait_recv()
        full = uinv[...].reshape(NB, NB)
        for t in range(rows // 256):
            lp[t * 256:(t + 1) * 256] = dot(m[t * 256:(t + 1) * 256, :NB], full).astype(BF16)
            for j in range(4 * t, 4 * t + 4):
                q = 2 if j >= 30 else j % 3
                for kk in range(2):
                    p_send(j, kk, q, 0, core(kk, (yp, ym, zp)[q])).start()
                    if q == 2:
                        sib_z_send(j - 20 if j >= 30 else j // 3, j, kk).start()
                    else:
                        sib_send(j, kk).start()

    zero = z == 0
    z35 = either(z == 3, z == 5)
    z_later = jnp.where(zero, 0, jnp.where(either(z == 1, z == 7), 3, jnp.where(z35, 7, 10)))
    start = []
    slots = []
    up = either(zero, either(z == 1, z35))
    up_to = (jnp.where(z == 1, zs[1], zs[0]), c)
    down = either(zero, either(z == 7, z == 3))
    down_to = (jnp.where(z == 7, zs[5], zs[6]), c)
    for q in range(2):
        near, far = (1, 3) if q == 0 else (3, 1)
        ahead, back = (yp, ym) if q == 0 else (ym, yp)
        at1 = y == near
        start.append(EARLY + z_later + jnp.where(at1, 0, jnp.where(y == far, 2 * HOP + LATE, jnp.where(y == 0, HOP + LATE, HOP))))
        slots.append([
            (either(at1, y == 2), ahead),
            (both(at1, z != 0), back),
            (both(at1, up), up_to),
            (both(at1, down), down_to),
        ])
    dy = jnp.minimum(y, 4 - y)
    on = both(y == 0, z != 0)
    start.append(EARLY - HOP + jnp.where(zero, 3 + (dy + 1) * HOP + LATE, z_later + dy * HOP + jnp.where(both(y == 2, z != 1), LATE, 0)))
    slots.append([
        (on, yp),
        (on, ym),
        (both(on, up), up_to),
        (either(both(on, down), both(y != 0, z == 1)), down_to),
        (both(either(y == 1, y == 3), z != 0), (jnp.where(y == 1, ys[0], ys[2]), c)),
    ])
    turn = jnp.where(y == 1, 0, 1)
    relay = r >= 2

    k_send = remote(linv.at[:, :, k], kss.at[0], krs.at[0], sib)

    steps = max(SOLVE * 7 + 6, EARLY + 10 + 2 * HOP + LATE + COUNT[2])

    @pl.loop(0, steps)
    def _(s):
        for t in range(1, 5):
            @pl.when(s == SOLVE * t + 1)
            def _(t=t):
                z_arrived(True, t).wait_recv()
                if t == 1:
                    pl.when(root)(z_block(False, 0).start)
                if t < 4:
                    z_block(True, t).start()
                    z_arrived(False, t).wait_recv()
                    if t < 3:
                        z_block(False, t).start()
                else:
                    y_slab(True, 0).start()
                    y_slab(False, 0).start()

        @pl.when(s == SOLVE * 5 + 1)
        def _():
            y_arrived(0).wait_recv()
            y_slab(True, 1).start()
            y_arrived(2).wait_recv()

        @pl.when(s == SOLVE * 6 + 1)
        def _():
            y_arrived(1).wait_recv()
            k_send.start()

        for h in range(2):
            n = s - X_AT - jnp.where(c == 2, HOP, 0)

            @pl.when(both(either(c == 2, c == (1 if h == 0 else 3)), both(n >= 0, n < N_X)))
            def _():
                copy = x_chunk(h, n)
                copy.wait_recv()
                copy.start()

        for q in range(3):
            ahead = s - start[q]
            n = ahead

            @pl.when(both(relay, both(n >= 0, n < COUNT[q])))
            def _():
                j = 3 * n + q if q < 2 else place(n)
                p_send(j, k, q, 0, yp).wait_recv()
                for slot, (cond, to) in enumerate(slots[q]):
                    if slot == 4:
                        cond = both(cond, n % 2 == turn)
                    pl.when(cond)(p_send(j, k, q, slot, to).start)
                sib_send(j, k).start()

        back = s - EARLY + 1

        @pl.when(both(r == 1, both(back >= 0, back < COUNT[2])))
        def _():
            n = back
            for kk in range(2):
                sib_z_send(n, place(n), kk).wait_recv()
                p_send(place(n), kk, 2, 0, other(zm) if kk == 0 else zm).start()

        @pl.when(s < rows // 256)
        def _():
            tile = pl.ds(pl.multiple_of(s * 256, 256), 256)
            ref[tile] = (m[tile].astype(F32) - dot(prev_l[tile], prev_u[...])).astype(BF16)

        @pl.when(s == SOLVE * 7 + 1)
        def _():
            remote(lp.at[pl.ds(0, 256)], kss.at[0], krs.at[0], sib).wait_recv()

        p = s - SOLVE * 7 - 2

        @pl.when(both(p >= 0, p < 4))
        def _():
            for h in range(2):
                @pl.when(c == (3 if h == 0 else 1))
                def _():
                    for i in range(4):
                        x_chunk(h, 4 * p + i).wait_recv()

            full_l = linv[...].reshape(NB, NB)
            ur[p] = dot(full_l, jnp.concatenate([r0[0, p], r0[1, p]], axis=1)).astype(BF16)

    @pl.when(relay)
    def _():
        remote(rows_of(32), pss.at[3, 0], prs2.at[0], sib).wait_recv()

    @pl.when(r == 1)
    def _():
        remote(rows_of(40), pss.at[3, 0], prs2.at[0], sib).wait_recv()
        remote(rows_of(24), pss.at[2, 0], prs.at[0], zm).wait_send()

    @pl.when(both(top, root))
    def _():
        ref[:NB, :NB] = m[:NB, :NB]

    remote(lp.at[pl.ds(0, 56)], zss.at[0], zrs.at[0], zp).wait_send()
    remote(lp.at[pl.ds(0, 192)], yss.at[0], yrs.at[0], yp).wait_send()
    k_send.wait_send()

    @pl.when(c <= 2)
    def _():
        remote(r0.at[0], xss.at[0], xrs.at[0, 0], xp).wait_send()

    @pl.when(c != 1)
    def _():
        remote(r0.at[1], xss.at[1], xrs.at[1, 0], xm).wait_send()

    @pl.when(root)
    def _():
        remote(lp.at[pl.ds(0, 384)], uss.at[0], urs.at[0], xp).wait_send()
        for q in range(3):
            remote(rows_of(2 * COUNT[q]), pss.at[q, 0], prs.at[0], yp).wait_send()
        remote(rows_of(40), pss.at[3, 0], prs2.at[0], sib).wait_send()
        remote(rows_of(24), pss.at[3, 1], prs2.at[0], sib).wait_send()

    @pl.when(relay)
    def _():
        for q in range(3):
            for slot, (cond, to) in enumerate(slots[q]):
                n = COUNT[q] // 2 if slot == 4 else COUNT[q]
                pl.when(cond)(remote(rows_of(n), pss.at[q, slot], prs.at[0], to).wait_send)
        remote(rows_of(32), pss.at[3, 0], prs2.at[0], sib).wait_send()


def finish(ref, lp, ur, out):
    t = pl.program_id(0)
    size = out.shape[0]
    root = lax.axis_index("row") == 0
    pivot = both(lax.axis_index("col") == 0, t < NB // size)
    tile = pl.ds(pl.multiple_of(t * size, size), size)

    def columns(p, h):
        return slice(h * 512 + p * 128, h * 512 + p * 128 + 128)

    @pl.when(pivot)
    def _():
        for p in range(4):
            for h in range(2):
                value = ur[p, tile, h * 128:(h + 1) * 128]
                if h == 0:
                    value = jnp.where(root, ref[tile, columns(p, h)], value)
                out[:, columns(p, h)] = value

    @pl.when(pivot == False)
    def _():
        left = lp[tile]
        for p in range(4):
            update = dot(left, ur[p])
            for h in range(2):
                part = update[:, h * 128:(h + 1) * 128]
                value = (ref[tile, columns(p, h)].astype(F32) - part).astype(BF16)
                if h == 0:
                    value = jnp.where(root, left[:, columns(p, 0)], value)
                out[:, columns(p, h)] = value


def local(*args):
    rows, cols = args[0].shape
    dma = pltpu.SemaphoreType.DMA
    hbm = pl.BlockSpec(memory_space=pl.ANY)
    vmem = pl.BlockSpec(memory_space=pltpu.VMEM)
    args = [pltpu.with_memory_space_constraint(a, pltpu.MemorySpace.HBM) for a in args]
    ref, lp, ur = pl.pallas_call(
        spread,
        name="spread",
        out_shape=(pltpu.VMEM((rows, cols), BF16), pltpu.VMEM((rows, NB), BF16), pltpu.VMEM((4, NB, 256), BF16)),
        in_specs=[hbm] * 5,
        out_specs=(vmem, vmem, vmem),
        scratch_shapes=[
            pltpu.VMEM((rows, cols), BF16),
            pltpu.VMEM((rows, NB), BF16),
            pltpu.VMEM((NB, cols), BF16),
            pltpu.VMEM((4, 8, 2, 8, NB), BF16),
            pltpu.VMEM((4, NB // 4, NB), BF16),
            pltpu.VMEM((2, 4, NB, 128), BF16),
            dma((7,)),
            dma((2,)),
            dma((2, N_X)),
            dma((4, 5)),
            dma((32,)),
            dma((1,)),
            dma((COUNT[2], 2)),
            dma((1,)), dma((2, 4)),
            dma((1,)), dma((3,)),
            dma((1,)), dma((1,)),
            dma((1,)), dma((1,)),
        ],
        compiler_params=pltpu.CompilerParams(collective_id=0, has_side_effects=True, vmem_limit_bytes=40 << 20),
        cost_estimate=pl.CostEstimate(flops=4 << 30, bytes_accessed=7 << 20, transcendentals=0),
    )(*args)
    size = 512
    return pl.pallas_call(
        finish,
        name="finish",
        grid=(rows // size,),
        out_shape=jax.ShapeDtypeStruct((rows, cols), BF16),
        in_specs=[vmem] * 3,
        out_specs=pl.BlockSpec((size, cols), lambda t: (t, 0)),
        compiler_params=pltpu.CompilerParams(vmem_limit_bytes=16 << 20),
        cost_estimate=pl.CostEstimate(flops=2 << 30, bytes_accessed=4 << 20, transcendentals=0),
    )(ref, lp, ur)


def solution(mesh):
    in_specs = (P("col", "row"), P("col", None), P(None, "row"), P("row", None), P("col", None))
    out_specs = P("col", "row")
    return jax.shard_map(local, mesh=mesh, in_specs=in_specs, out_specs=out_specs, check_vma=False)
```

```python
import jax
import jax.numpy as jnp
from jax import lax
from jax.experimental import pallas as pl
from jax.experimental.pallas import tpu as pltpu
from jax.sharding import PartitionSpec as P

MESH = pl.DeviceIdType.MESH
NB = 512
CH = 32
HOP = 4
EARLY = 2
LATE = 2
SOLVE = 4
X_AT = 3
COUNT = (10, 10, 12)
N_X = 16
F32 = jnp.float32
BF16 = jnp.bfloat16


def dot(a, b):
    return jnp.dot(a, b, preferred_element_type=F32)


def both(a, b):
    return jnp.logical_and(a, b)


def either(a, b):
    return jnp.logical_or(a, b)


def remote(src, send, recv, to):
    return pltpu.make_async_remote_copy(src_ref=src, dst_ref=src, send_sem=send, recv_sem=recv,
                                        device_id=to, device_id_type=MESH)


def spread(m_hbm, pl_hbm, pu_hbm, li_hbm, ui_hbm, ref, lp, ur,
           m, prev_l, prev_u, linv, uinv, r0,
           in_sem, xss, xrs, pss, prs, prs2, prs3, zss, zrs, yss, yrs, kss, krs, uss, urs):
    rows = m.shape[0]
    r = lax.axis_index("row")
    c = lax.axis_index("col")
    y, z, k = r // 16, (r // 2) % 8, r % 2
    top = c == 0
    root = r == 0
    root_chip = r < 2

    own_l = linv.at[y, z, k]
    loads = [pltpu.make_async_copy(src, dst, in_sem.at[i]) for i, (src, dst) in enumerate((
        (li_hbm, own_l),
        (ui_hbm, uinv.at[c]),
        (pu_hbm, prev_u),
        (pl_hbm.at[pl.ds(0, NB)], prev_l.at[pl.ds(0, NB)]),
        (m_hbm.at[pl.ds(0, NB)], m.at[pl.ds(0, NB)]),
        (m_hbm.at[pl.ds(NB, rows - NB)], m.at[pl.ds(NB, rows - NB)]),
        (pl_hbm.at[pl.ds(NB, rows - NB)], prev_l.at[pl.ds(NB, rows - NB)]),
    ))]
    for load in loads:
        load.start()

    zs = [r + 2 * d - 16 * ((z + d) // 8) for d in range(1, 8)]
    ys = [r + 16 * d - 64 * ((y + d) // 4) for d in range(1, 4)]
    xs = [(c + d) % 4 for d in range(1, 4)]
    sib = (r + 1 - 2 * k, c)
    zp, zp2, zm2, zm = (zs[0], c), (zs[1], c), (zs[5], c), (zs[6], c)
    yp, ym = (ys[0], c), (ys[2], c)
    xp, xm = (r, xs[0]), (r, xs[2])

    def other(at):
        return (at[0] + 1 - 2 * k, c)

    barrier = pltpu.get_barrier_semaphore()

    def greet(at):
        pl.semaphore_signal(barrier, inc=1, device_id=at, device_id_type=MESH)

    for at in [zp, zm, yp, ym, sib] + [(r, a) for a in xs]:
        if at is zp:
            pl.when(zs[0] != 0)(lambda: greet(zp))
        else:
            greet(at)
    pl.when(z == 3)(lambda: greet(zm2))
    pl.when(z == 5)(lambda: greet(zp2))
    at_root = (0, c)
    for a in (3, 17, 49):
        pl.when(r == a)(lambda: greet(at_root))
    pl.when(r == 14)(lambda: greet((1, c)))
    count = 8 + jnp.where(either(z == 1, z == 7), 1, 0)
    count = jnp.where(root, 10, jnp.where(r == 1, 9, count))
    pl.semaphore_wait(barrier, count)

    loads[0].wait()
    loads[1].wait()

    def z_block(up, t):
        part = linv.at[y, (z - t) % 8 if up else (z + t) % 8, k]
        return remote(part, zss.at[0], zrs.at[0 if up else 1, t], zp if up else zm)

    def z_arrived(up, t):
        return remote(own_l, zss.at[0], zrs.at[0 if up else 1, t - 1], zp)

    def y_slab(up, t):
        part = linv.at[(y - t) % 4, :, k]
        return remote(part, yss.at[0], yrs.at[t if up else 2], yp if up else ym)

    def y_arrived(i):
        return remote(lp.at[pl.ds(0, 64)], yss.at[0], yrs.at[i], yp)

    z_block(True, 0).start()
    pl.when(r != 0)(z_block(False, 0).start)
    u_sends = [remote(uinv.at[c], uss.at[0], urs.at[0], (r, a)) for a in xs]

    @pl.when(root)
    def _():
        for copy in u_sends:
            copy.start()

    def x_chunk(h, n):
        part = r0.at[h, n // 4, pl.ds(pl.multiple_of((n % 4) * 128, 128), 128)]
        return remote(part, xss.at[h], xrs.at[h, n], xp if h == 0 else xm)

    for load in loads[2:5]:
        load.wait()

    @pl.when(top)
    def _():
        for p in range(4):
            cols = [slice(h * 512 + p * 128, h * 512 + p * 128 + 128) for h in range(2)]
            product = dot(prev_l[:NB], jnp.concatenate([prev_u[:, a] for a in cols], axis=1))
            for h in range(2):
                part = product[:, h * 128:(h + 1) * 128]
                r0[h, p] = (m[:NB, cols[h]].astype(F32) - part).astype(BF16)
            for i in range(4):
                for h in range(2):
                    x_chunk(h, 4 * p + i).start()

    for load in loads[5:]:
        load.wait()

    def p_chunk(j, kk):
        return lp.at[pl.ds(pl.multiple_of((2 * j + kk) * CH, CH), CH)]

    def p_send(j, kk, q, slot, to):
        return remote(p_chunk(j, kk), pss.at[q, slot], prs.at[j], to)

    def sib_send(j, kk):
        return remote(p_chunk(j, kk), pss.at[3, 0], prs2.at[0], sib)

    def sib_z_send(n, j, kk):
        return remote(p_chunk(j, kk), pss.at[3, 1], prs3.at[n, kk], sib)

    def place(n):
        return jnp.where(n < 10, 3 * n + 2, n + 20)

    def rows_of(n):
        return lp.at[pl.ds(0, n * CH)]

    def core(kk, at):
        return at if kk == 0 else other(at)

    @pl.when(root)
    def _():
        remote(lp.at[pl.ds(0, 384)], uss.at[0], urs.at[0], xp).wait_recv()
        full = uinv[...].reshape(NB, NB)
        for t in range(rows // 256):
            lp[t * 256:(t + 1) * 256] = dot(m[t * 256:(t + 1) * 256, :NB], full).astype(BF16)
            for j in range(4 * t, 4 * t + 4):
                q = 2 if j >= 30 else j % 3
                for kk in range(2):
                    p_send(j, kk, q, 0, core(kk, (yp, ym, zp)[q])).start()
                    if q == 2:
                        sib_z_send(j - 20 if j >= 30 else j // 3, j, kk).start()
        for j in range(30):
            for kk in range(2):
                if j % 3 != 2:
                    sib_send(j, kk).start()

    zero = z == 0
    z35 = either(z == 3, z == 5)
    z_later = jnp.where(zero, 0, jnp.where(either(z == 1, z == 7), 3, jnp.where(z35, 7, 10)))
    start = []
    slots = []
    up = either(zero, either(z == 1, z35))
    up_to = (jnp.where(z == 1, zs[1], zs[0]), c)
    down = either(zero, either(z == 7, z == 3))
    down_to = (jnp.where(z == 7, zs[5], zs[6]), c)
    for q in range(2):
        near, far = (1, 3) if q == 0 else (3, 1)
        ahead, back = (yp, ym) if q == 0 else (ym, yp)
        at1 = y == near
        start.append(EARLY + z_later + jnp.where(at1, 0, jnp.where(y == far, 2 * HOP + LATE, jnp.where(y == 0, HOP + LATE, HOP))))
        slots.append([
            (either(at1, y == 2), ahead),
            (both(at1, z != 0), back),
            (both(at1, up), up_to),
            (both(at1, down), down_to),
        ])
    dy = jnp.minimum(y, 4 - y)
    on = both(y == 0, z != 0)
    start.append(EARLY - HOP + jnp.where(zero, 3 + (dy + 1) * HOP + LATE, z_later + dy * HOP + jnp.where(both(y == 2, z != 1), LATE, 0)))
    slots.append([
        (on, yp),
        (on, ym),
        (both(on, up), up_to),
        (either(both(on, down), both(y != 0, z == 1)), down_to),
        (both(either(y == 1, y == 3), z != 0), (jnp.where(y == 1, ys[0], ys[2]), c)),
    ])
    turn = jnp.where(y == 1, 0, 1)
    relay = r >= 2

    k_send = remote(linv.at[:, :, k], kss.at[0], krs.at[0], sib)

    steps = max(SOLVE * 7 + 6, EARLY + 10 + 2 * HOP + LATE + COUNT[2])

    @pl.loop(0, steps)
    def _(s):
        for t in range(1, 5):
            @pl.when(s == SOLVE * t + 1)
            def _(t=t):
                z_arrived(True, t).wait_recv()
                if t == 1:
                    pl.when(root)(z_block(False, 0).start)
                if t < 4:
                    z_block(True, t).start()
                    z_arrived(False, t).wait_recv()
                    if t < 3:
                        z_block(False, t).start()
                else:
                    y_slab(True, 0).start()
                    y_slab(False, 0).start()

        @pl.when(s == SOLVE * 5 + 1)
        def _():
            y_arrived(0).wait_recv()
            y_slab(True, 1).start()
            y_arrived(2).wait_recv()

        @pl.when(s == SOLVE * 6 + 1)
        def _():
            y_arrived(1).wait_recv()
            k_send.start()

        for h in range(2):
            n = s - X_AT - jnp.where(c == 2, HOP, 0)

            @pl.when(both(either(c == 2, c == (1 if h == 0 else 3)), both(n >= 0, n < N_X)))
            def _():
                copy = x_chunk(h, n)
                copy.wait_recv()
                copy.start()

        for q in range(3):
            ahead = s - start[q]
            n = ahead

            @pl.when(both(relay, both(n >= 0, n < COUNT[q])))
            def _():
                j = 3 * n + q if q < 2 else place(n)
                p_send(j, k, q, 0, yp).wait_recv()
                for slot, (cond, to) in enumerate(slots[q]):
                    if slot == 4:
                        cond = both(cond, n % 2 == turn)
                    pl.when(cond)(p_send(j, k, q, slot, to).start)
                sib_send(j, k).start()

        back = s - EARLY + 1

        @pl.when(both(r == 1, both(back >= 0, back < COUNT[2])))
        def _():
            n = back
            for kk in range(2):
                sib_z_send(n, place(n), kk).wait_recv()
                p_send(place(n), kk, 2, 0, other(zm) if kk == 0 else zm).start()

        @pl.when(s < rows // 256)
        def _():
            tile = pl.ds(pl.multiple_of(s * 256, 256), 256)
            ref[tile] = (m[tile].astype(F32) - dot(prev_l[tile], prev_u[...])).astype(BF16)

        @pl.when(s == SOLVE * 7 + 1)
        def _():
            remote(lp.at[pl.ds(0, 256)], kss.at[0], krs.at[0], sib).wait_recv()

        p = s - SOLVE * 7 - 2

        @pl.when(both(p >= 0, p < 4))
        def _():
            for h in range(2):
                @pl.when(c == (3 if h == 0 else 1))
                def _():
                    for i in range(4):
                        x_chunk(h, 4 * p + i).wait_recv()

            full_l = linv[...].reshape(NB, NB)
            ur[p] = dot(full_l, jnp.concatenate([r0[0, p], r0[1, p]], axis=1)).astype(BF16)

    @pl.when(relay)
    def _():
        remote(rows_of(32), pss.at[3, 0], prs2.at[0], sib).wait_recv()

    @pl.when(r == 1)
    def _():
        remote(rows_of(40), pss.at[3, 0], prs2.at[0], sib).wait_recv()
        remote(rows_of(24), pss.at[2, 0], prs.at[0], zm).wait_send()

    @pl.when(both(top, root))
    def _():
        ref[:NB, :NB] = m[:NB, :NB]

    remote(lp.at[pl.ds(0, 56)], zss.at[0], zrs.at[0], zp).wait_send()
    remote(lp.at[pl.ds(0, 192)], yss.at[0], yrs.at[0], yp).wait_send()
    k_send.wait_send()

    @pl.when(c <= 2)
    def _():
        remote(r0.at[0], xss.at[0], xrs.at[0, 0], xp).wait_send()

    @pl.when(c != 1)
    def _():
        remote(r0.at[1], xss.at[1], xrs.at[1, 0], xm).wait_send()

    @pl.when(root)
    def _():
        remote(lp.at[pl.ds(0, 384)], uss.at[0], urs.at[0], xp).wait_send()
        for q in range(3):
            remote(rows_of(2 * COUNT[q]), pss.at[q, 0], prs.at[0], yp).wait_send()
        remote(rows_of(40), pss.at[3, 0], prs2.at[0], sib).wait_send()
        remote(rows_of(24), pss.at[3, 1], prs2.at[0], sib).wait_send()

    @pl.when(relay)
    def _():
        for q in range(3):
            for slot, (cond, to) in enumerate(slots[q]):
                n = COUNT[q] // 2 if slot == 4 else COUNT[q]
                pl.when(cond)(remote(rows_of(n), pss.at[q, slot], prs.at[0], to).wait_send)
        remote(rows_of(32), pss.at[3, 0], prs2.at[0], sib).wait_send()


def finish(ref, lp, ur, out):
    t = pl.program_id(0)
    size = out.shape[0]
    root = lax.axis_index("row") == 0
    pivot = both(lax.axis_index("col") == 0, t < NB // size)
    tile = pl.ds(pl.multiple_of(t * size, size), size)

    def columns(p, h):
        return slice(h * 512 + p * 128, h * 512 + p * 128 + 128)

    @pl.when(pivot)
    def _():
        for p in range(4):
            for h in range(2):
                value = ur[p, tile, h * 128:(h + 1) * 128]
                if h == 0:
                    value = jnp.where(root, ref[tile, columns(p, h)], value)
                out[:, columns(p, h)] = value

    @pl.when(pivot == False)
    def _():
        left = lp[tile]
        for p in range(4):
            update = dot(left, ur[p])
            for h in range(2):
                part = update[:, h * 128:(h + 1) * 128]
                value = (ref[tile, columns(p, h)].astype(F32) - part).astype(BF16)
                if h == 0:
                    value = jnp.where(root, left[:, columns(p, 0)], value)
                out[:, columns(p, h)] = value


def local(*args):
    rows, cols = args[0].shape
    dma = pltpu.SemaphoreType.DMA
    hbm = pl.BlockSpec(memory_space=pl.ANY)
    vmem = pl.BlockSpec(memory_space=pltpu.VMEM)
    args = [pltpu.with_memory_space_constraint(a, pltpu.MemorySpace.HBM) for a in args]
    ref, lp, ur = pl.pallas_call(
        spread,
        name="spread",
        out_shape=(pltpu.VMEM((rows, cols), BF16), pltpu.VMEM((rows, NB), BF16), pltpu.VMEM((4, NB, 256), BF16)),
        in_specs=[hbm] * 5,
        out_specs=(vmem, vmem, vmem),
        scratch_shapes=[
            pltpu.VMEM((rows, cols), BF16),
            pltpu.VMEM((rows, NB), BF16),
            pltpu.VMEM((NB, cols), BF16),
            pltpu.VMEM((4, 8, 2, 8, NB), BF16),
            pltpu.VMEM((4, NB // 4, NB), BF16),
            pltpu.VMEM((2, 4, NB, 128), BF16),
            dma((7,)),
            dma((2,)),
            dma((2, N_X)),
            dma((4, 5)),
            dma((32,)),
            dma((1,)),
            dma((COUNT[2], 2)),
            dma((1,)), dma((2, 4)),
            dma((1,)), dma((3,)),
            dma((1,)), dma((1,)),
            dma((1,)), dma((1,)),
        ],
        compiler_params=pltpu.CompilerParams(collective_id=0, has_side_effects=True, vmem_limit_bytes=40 << 20),
        cost_estimate=pl.CostEstimate(flops=4 << 30, bytes_accessed=7 << 20, transcendentals=0),
    )(*args)
    size = 512
    return pl.pallas_call(
        finish,
        name="finish",
        grid=(rows // size,),
        out_shape=jax.ShapeDtypeStruct((rows, cols), BF16),
        in_specs=[vmem] * 3,
        out_specs=pl.BlockSpec((size, cols), lambda t: (t, 0)),
        compiler_params=pltpu.CompilerParams(vmem_limit_bytes=16 << 20),
        cost_estimate=pl.CostEstimate(flops=2 << 30, bytes_accessed=4 << 20, transcendentals=0),
    )(ref, lp, ur)


def solution(mesh):
    in_specs = (P("col", "row"), P("col", None), P(None, "row"), P("row", None), P("col", None))
    out_specs = P("col", "row")
    return jax.shard_map(local, mesh=mesh, in_specs=in_specs, out_specs=out_specs, check_vma=False)
```
